32 devices in a mesh: rows: 8 (over y, x, core), cols: 4 (over z).
Axes of the slice: x: 2, y: 2, z: 4, core: 2. Of those that a mesh axis runs over, the one named last changes fastest.
Arguments:
- up_a: bfloat16 [28672, 4096], P('rows', 'cols'), may hold values from -6 to 6
- gate_a: bfloat16 [28672, 4096], P('rows', 'cols'), may hold values from -6 to 6
- down_a: bfloat16 [28672, 4096], P('rows', 'cols'), may hold values from -6 to 6
- up_b: bfloat16 [28672, 4096], P('rows', 'cols'), may hold values from -6 to 6
- gate_b: bfloat16 [28672, 4096], P('rows', 'cols'), may hold values from -6 to 6
- down_b: bfloat16 [28672, 4096], P('rows', 'cols'), may hold values from -6 to 6
- perm: int32 [28672], P('rows'), may hold values from 0 to 28671, as said below
Outputs:
- costs: float32 [28672, 256], P('rows', 'cols')
- up_mean: bfloat16 [28672, 4096], P('rows', 'cols')
- gate_mean: bfloat16 [28672, 4096], P('rows', 'cols')
- down_mean: bfloat16 [28672, 4096], P('rows', 'cols')
The draws below stay inside these ranges and needn't reach their ends.
Inputs may be any that keep to these rules, and one draw needn't show every extreme that they name: perm is a permutation of the hidden units. Split positions and values alike into aligned blocks of 3584: the positions of one block take at most 448 values from any one block, and exactly 448 from some block.
All inputs are finite; a program needn't handle non-finite values.
Results may differ from the reference program's by a relative error of at most 0.001.
Values may be sent and summed in bfloat16 or wider, within the bound.
A program may use at most 192 MiB of HBM per device.

```python
import jax
import jax.numpy as jnp
from jax import lax

D = 4096
FF = 28672
BLOCKS = 8
FF_DEV = 3584
WIN = 256
STRIDE = 112
CAP = 448
N_ROWS = 8


def draw_perm(key, part):
    peers = N_ROWS
    row_count = FF_DEV
    capacity = CAP
    key_offset, key_rest, key_rows, key_order = jax.random.split(key, 4)
    offset_dev = jax.random.randint(key_offset, (), 0, peers).astype(jnp.int32)
    spare_rows = row_count - capacity
    rounds = max(1, (spare_rows + peers - 2) // (peers - 1))
    round_keys = jax.random.split(key_rest, rounds)
    others = jax.vmap(lambda one_key: jax.random.permutation(one_key, peers - 1))(round_keys)
    others = others.reshape(-1)[:spare_rows].astype(jnp.int32)
    shifts = jnp.concatenate([jnp.full((capacity,), 0, jnp.int32) + offset_dev, (offset_dev + 1 + others) % peers])
    local_rows = jax.random.permutation(key_rows, row_count).astype(jnp.int32)
    order_keys = jax.random.split(key_order, peers)
    orders = jax.vmap(lambda one_key: jax.random.permutation(one_key, row_count))(order_keys).astype(jnp.int32)
    blocks = jnp.arange(peers, dtype=jnp.int32)[:, None]
    source = (blocks + shifts[orders]) % peers
    return (source * row_count + local_rows[orders]).reshape(-1).astype(jnp.int32)


def shard_levels(key, shape, cuts, smallest, largest):
    level, own = 1.0, jax.random.fold_in(key, 6)
    for axis_at, shards_of in cuts:
        draws = jnp.exp(jax.random.uniform(jax.random.fold_in(own, axis_at), (shards_of,), jnp.float32, smallest / len(cuts), largest / len(cuts)))
        level = level * jnp.repeat(draws, shape[axis_at] // shards_of).reshape([-1 if axis == axis_at else 1 for axis in range(len(shape))])
    return level


def normal_values(rng, dims, spread, reach, cuts=(), kind=jnp.bfloat16):
    array = jax.random.normal(rng, dims, jnp.float32) * spread
    if len(cuts) > 0:
        array = shard_levels(rng, dims, cuts, -0.22, 0.18) * array
    return jnp.clip(array, min=-reach, max=reach).astype(kind)


def setup_inputs(seed: int = 0) -> dict:
    streams_of = jax.random.split(jax.random.key(seed), 8)
    up_a = normal_values(streams_of[0], (FF, D), 1.0, 6.0, ((0, 8), (1, 4)))
    gate_a = normal_values(streams_of[1], (FF, D), 1.0, 6.0, ((0, 8), (1, 4)))
    down_a = normal_values(streams_of[2], (FF, D), 1.0, 6.0, ((0, 8), (1, 4)))
    up_b = normal_values(streams_of[3], (FF, D), 1.0, 6.0, ((0, 8), (1, 4)))
    gate_b = normal_values(streams_of[4], (FF, D), 1.0, 6.0, ((0, 8), (1, 4)))
    down_b = normal_values(streams_of[5], (FF, D), 1.0, 6.0, ((0, 8), (1, 4)))
    perm = draw_perm(jax.random.fold_in(streams_of[7], 71), 0)
    return dict(up_a=up_a, gate_a=gate_a, down_a=down_a, up_b=up_b, gate_b=gate_b, down_b=down_b, perm=perm)


def reference(up_a, gate_a, down_a, up_b, gate_b, down_b, perm):
    columns = jnp.arange(WIN, dtype=jnp.int32)
    window_neurons = (columns % BLOCKS) * FF_DEV + (columns // BLOCKS) * STRIDE
    window_up = up_a[window_neurons].astype(jnp.float32)
    window_gate = gate_a[window_neurons].astype(jnp.float32)
    cost_scale = (2.0 * D) ** -0.5
    costs = jnp.dot(up_b.astype(jnp.float32), window_up.T, precision=lax.Precision.HIGHEST)
    costs = costs + jnp.dot(gate_b.astype(jnp.float32), window_gate.T, precision=lax.Precision.HIGHEST)
    costs = costs * cost_scale
    results = []
    for initial, other in ((up_a, up_b), (gate_a, gate_b), (down_a, down_b)):
        matched = other[perm].astype(jnp.float32)
        results.append(((initial.astype(jnp.float32) + matched) * 0.5).astype(jnp.bfloat16))
    return (costs, results[0], results[1], results[2])
```

```python
import jax
import jax.numpy as jnp
from jax import lax
from jax.sharding import PartitionSpec as P

D = 4096
A_DEV = 32


def rows_gather(window):
    peers = lax.axis_size("rows")
    me = lax.axis_index("rows")
    held = window
    reach = 1
    while reach < peers:
        other = lax.ppermute(held, "rows", [(r, r ^ reach) for r in range(peers)])
        upper = (me // reach) % 2 == 1
        held = jnp.concatenate(
            [jnp.where(upper, other, held), jnp.where(upper, held, other)], axis=1
        )
        reach *= 2
    return held


def cols_reduce(parts):
    count = lax.axis_size("cols")
    me = lax.axis_index("cols")
    total = lax.dynamic_index_in_dim(parts, me, 0, keepdims=False)
    for shift in range(1, count):
        piece = lax.dynamic_index_in_dim(parts, (me + shift) % count, 0, keepdims=False)
        total = total + lax.ppermute(piece, "cols", [(c, (c + shift) % count) for c in range(count)])
    return total


def pick(array, index):
    return array.at[index].get(mode="promise_in_bounds")


def mix(initial, picked):
    return ((initial.astype(jnp.float32) + picked.astype(jnp.float32)) * 0.5).astype(jnp.bfloat16)


def local(up_a, gate_a, down_a, up_b, gate_b, down_b, perm):
    row_count = up_a.shape[0]
    features = up_a.shape[1]
    stride = row_count // A_DEV
    cost_scale = (2.0 * D) ** (-0.5)
    peers = lax.axis_size("rows")
    cols = lax.axis_size("cols")
    capacity = max(2, (row_count + peers - 1) // peers)

    source = perm // row_count
    local_row = perm % row_count
    blocks = jnp.arange(peers, dtype=jnp.int32)
    matches = (source[None, :] == blocks[:, None]).astype(jnp.int32)
    arrival_rank = jnp.sum(jnp.cumsum(matches, axis=1) * matches, axis=0) - 1
    high = (local_row // 256).astype(jnp.bfloat16)
    low = (local_row % 256).astype(jnp.bfloat16)
    halves = jnp.stack([high, low])[:, None, :] * matches.astype(jnp.bfloat16)[None]
    at_rank = (arrival_rank[None, :] == jnp.arange(capacity, dtype=jnp.int32)[:, None]).astype(jnp.bfloat16)
    found = jnp.einsum("hsi,ri->hsr", halves, at_rank, preferred_element_type=jnp.float32)
    wanted = found[0].astype(jnp.int32) * 256 + found[1].astype(jnp.int32)
    asked_rows = lax.all_to_all(wanted, "rows", split_axis=0, concat_axis=0, tiled=True)

    def exchange(array, index):
        return lax.all_to_all(pick(array, index), "rows", split_axis=0, concat_axis=0, tiled=True)

    window = jnp.stack([up_a[::stride], gate_a[::stride]])
    pieces = rows_gather(window[:, None])
    wide = pieces.transpose(0, 2, 1, 3).reshape(2, A_DEV * peers, features)
    partial_value = jnp.einsum("kd,jd->kj", wide[0], up_b, preferred_element_type=jnp.float32)
    partial_value = partial_value + jnp.einsum(
        "kd,jd->kj", wide[1], gate_b, preferred_element_type=jnp.float32
    )
    total = cols_reduce(partial_value.reshape(cols, -1, row_count))
    costs_out = (total * cost_scale).T

    first = capacity // 4 // 16 * 16
    if first > 0:
        early = exchange(up_b, asked_rows[:, :first])
        late = exchange(up_b, asked_rows[:, first:])
        held = jnp.concatenate(
            [early.reshape(peers * first, features), late.reshape(-1, features)], axis=0
        )
        slot_split = jnp.where(
            arrival_rank < first,
            source * first + arrival_rank,
            peers * first + source * (capacity - first) + arrival_rank - first,
        )
    else:
        held = exchange(up_b, asked_rows).reshape(-1, features)
        slot_split = source * capacity + arrival_rank
    slot = source * capacity + arrival_rank
    up_mean = mix(up_a, pick(held, slot_split))
    gate_moved = exchange(gate_b, asked_rows)
    gate_moved, up_mean = lax.optimization_barrier((gate_moved, up_mean))
    gate_mean = mix(gate_a, pick(gate_moved.reshape(-1, features), slot))

    cut = features * 3 // 4 // 128 * 128
    left = exchange(down_b[:, :cut], asked_rows)
    left, gate_mean = lax.optimization_barrier((left, gate_mean))
    left_mean = mix(down_a[:, :cut], pick(left.reshape(-1, cut), slot))
    down_mean = lax.dynamic_update_slice(jnp.zeros_like(down_a), left_mean, (0, 0))
    right = exchange(down_b[:, cut:], asked_rows)
    right, down_mean = lax.optimization_barrier((right, down_mean))
    right_mean = mix(down_a[:, cut:], pick(right.reshape(-1, features - cut), slot))
    down_mean = lax.dynamic_update_slice(down_mean, right_mean, (0, cut))
    return (costs_out, up_mean, gate_mean, down_mean)


def solution(mesh):
    placed = (P("rows", "cols"),) * 6 + (P("rows"),)
    return jax.shard_map(
        local,
        mesh=mesh,
        in_specs=placed,
        out_specs=(P("rows", "cols"),) * 4,
        check_vma=False,
    )
```

```python
import jax
import jax.numpy as jnp
from jax import lax
from jax.sharding import PartitionSpec as P

D = 4096
A_DEV = 32


def rows_gather(window):
    peers = lax.axis_size("rows")
    me = lax.axis_index("rows")
    held = window[:, :, None]
    reach = peers // 2
    while reach >= 1:
        other = lax.ppermute(held, "rows", [(r, r ^ reach) for r in range(peers)])
        upper = (me // reach) % 2 == 1
        pair = jnp.stack([jnp.where(upper, other, held), jnp.where(upper, held, other)], axis=3)
        held = pair.reshape(pair.shape[0], pair.shape[1], -1, pair.shape[4])
        reach //= 2
    return held


def cols_reduce(parts):
    count = lax.axis_size("cols")
    me = lax.axis_index("cols")
    moved = [lax.dynamic_index_in_dim(parts, me, 0, keepdims=False)]
    for shift in range(1, count):
        piece = lax.dynamic_index_in_dim(parts, (me + shift) % count, 0, keepdims=False)
        moved.append(lax.ppermute(piece, "cols", [(c, (c + shift) % count) for c in range(count)]))
    return moved


def pick(array, index):
    return array.at[index].get(mode="promise_in_bounds")


def mix(initial, picked):
    return ((initial.astype(jnp.float32) + picked.astype(jnp.float32)) * 0.5).astype(jnp.bfloat16)


def local(up_a, gate_a, down_a, up_b, gate_b, down_b, perm):
    row_count = up_a.shape[0]
    features = up_a.shape[1]
    stride = row_count // A_DEV
    cost_scale = (2.0 * D) ** (-0.5)
    peers = lax.axis_size("rows")
    cols = lax.axis_size("cols")
    capacity = max(2, (row_count + peers - 1) // peers)

    source = perm // row_count
    local_row = perm % row_count
    blocks = jnp.arange(peers, dtype=jnp.int32)
    matches = (source[None, :] == blocks[:, None]).astype(jnp.int32)
    arrival_rank = jnp.sum(jnp.cumsum(matches, axis=1) * matches, axis=0) - 1
    high = (local_row // 256).astype(jnp.bfloat16)
    low = (local_row % 256).astype(jnp.bfloat16)
    halves = jnp.stack([high, low])[:, None, :] * matches.astype(jnp.bfloat16)[None]
    at_rank = (arrival_rank[None, :] == jnp.arange(capacity, dtype=jnp.int32)[:, None]).astype(jnp.bfloat16)
    found = jnp.einsum("hsi,ri->hsr", halves, at_rank, preferred_element_type=jnp.float32)
    wanted = found[0].astype(jnp.int32) * 256 + found[1].astype(jnp.int32)
    asked_rows = lax.all_to_all(wanted, "rows", split_axis=0, concat_axis=0, tiled=True)

    def exchange(rows):
        moved = rows.reshape(peers, -1, rows.shape[1])
        moved = lax.all_to_all(moved, "rows", split_axis=0, concat_axis=0, tiled=True)
        return moved.reshape(-1, rows.shape[1])

    asked = asked_rows.reshape(-1)
    slot = source * capacity + arrival_rank

    pieces = rows_gather(jnp.stack([up_a[::stride], gate_a[::stride]]))
    wide = pieces.reshape(2, A_DEV * peers, features)

    up_rows = pick(up_b, asked)
    up_rows, wide = lax.optimization_barrier((up_rows, wide))
    up_moved = exchange(up_rows)

    partial_value = jnp.einsum("kd,jd->kj", wide[0], up_b, preferred_element_type=jnp.float32)
    partial_value = partial_value + jnp.einsum(
        "kd,jd->kj", wide[1], gate_b, preferred_element_type=jnp.float32
    )
    gate_rows = pick(gate_b, asked)
    gate_rows, partial_value = lax.optimization_barrier((gate_rows, partial_value))
    terms = cols_reduce(partial_value.reshape(cols, -1, row_count))

    cut = features * 3 // 4 // 128 * 128
    left_rows = pick(down_b[:, :cut], asked)
    right_rows = pick(down_b[:, cut:], asked)

    gate_moved = exchange(gate_rows)
    up_mean = mix(up_a, pick(up_moved, slot))
    tied = lax.optimization_barrier((left_rows, right_rows, up_mean) + tuple(terms[1::2]))
    left_rows, right_rows, up_mean = tied[:3]
    terms[1::2] = tied[3:]
    left = exchange(left_rows)
    gate_mean = mix(gate_a, pick(gate_moved, slot))
    tied = lax.optimization_barrier((right_rows, gate_mean) + tuple(terms[::2]))
    right_rows, gate_mean = tied[:2]
    terms[::2] = tied[2:]
    right = exchange(right_rows)
    left_mean = mix(down_a[:, :cut], pick(left, slot))
    down_mean = lax.dynamic_update_slice(jnp.zeros_like(down_a), left_mean, (0, 0))
    total = terms[0]
    for term in terms[1:]:
        total = total + term
    costs_out = (total * cost_scale).T
    right, down_mean, costs_out = lax.optimization_barrier((right, down_mean, costs_out))
    right_mean = mix(down_a[:, cut:], pick(right, slot))
    down_mean = lax.dynamic_update_slice(down_mean, right_mean, (0, cut))
    return (costs_out, up_mean, gate_mean, down_mean)


def solution(mesh):
    placed = (P("rows", "cols"),) * 6 + (P("rows"),)
    return jax.shard_map(
        local,
        mesh=mesh,
        in_specs=placed,
        out_specs=(P("rows", "cols"),) * 4,
        check_vma=False,
    )
```

```python
import jax
import jax.numpy as jnp
from jax import lax
from jax.sharding import PartitionSpec as P

D = 4096
A_DEV = 32


def cols_reduce(parts):
    count = lax.axis_size("cols")
    me = lax.axis_index("cols")
    moved = [lax.dynamic_index_in_dim(parts, me, 0, keepdims=False)]
    for shift in range(1, count):
        piece = lax.dynamic_index_in_dim(parts, (me + shift) % count, 0, keepdims=False)
        moved.append(lax.ppermute(piece, "cols", [(c, (c + shift) % count) for c in range(count)]))
    return moved


def pick(array, index):
    return array.at[index].get(mode="promise_in_bounds")


def mix(initial, picked):
    return ((initial.astype(jnp.float32) + picked.astype(jnp.float32)) * 0.5).astype(jnp.bfloat16)


def local(up_a, gate_a, down_a, up_b, gate_b, down_b, perm):
    row_count = up_a.shape[0]
    features = up_a.shape[1]
    stride = row_count // A_DEV
    cost_scale = (2.0 * D) ** (-0.5)
    peers = lax.axis_size("rows")
    cols = lax.axis_size("cols")
    capacity = max(2, (row_count + peers - 1) // peers)

    source = perm // row_count
    local_row = perm % row_count
    blocks = jnp.arange(peers, dtype=jnp.int32)
    matches = (source[None, :] == blocks[:, None]).astype(jnp.int32)
    arrival_rank = jnp.sum(jnp.cumsum(matches, axis=1) * matches, axis=0) - 1
    high = (local_row // 256).astype(jnp.bfloat16)
    low = (local_row % 256).astype(jnp.bfloat16)
    halves = jnp.stack([high, low])[:, None, :] * matches.astype(jnp.bfloat16)[None]
    at_rank = (arrival_rank[None, :] == jnp.arange(capacity, dtype=jnp.int32)[:, None]).astype(jnp.bfloat16)
    found = jnp.einsum("hsi,ri->hsr", halves, at_rank, preferred_element_type=jnp.float32)
    wanted = found[0].astype(jnp.int32) * 256 + found[1].astype(jnp.int32)
    wanted, up_held, gate_held = lax.optimization_barrier((wanted, up_a, gate_a))
    window = jnp.concatenate([up_held[::stride], gate_held[::stride]], axis=0)
    asked_rows = lax.all_to_all(wanted, "rows", split_axis=0, concat_axis=0, tiled=True)

    def exchange(rows):
        moved = rows.reshape(peers, -1, rows.shape[1])
        moved = lax.all_to_all(moved, "rows", split_axis=0, concat_axis=0, tiled=True)
        return moved.reshape(-1, rows.shape[1])

    asked = asked_rows.reshape(-1)
    slot = source * capacity + arrival_rank

    asked, window = lax.optimization_barrier((asked, window))
    sent = jnp.broadcast_to(window[None], (peers,) + window.shape)
    pieces = lax.all_to_all(sent, "rows", split_axis=0, concat_axis=0, tiled=True)
    up_rows = pick(up_b, asked)
    up_rows, pieces = lax.optimization_barrier((up_rows, pieces))
    up_moved = exchange(up_rows)
    pieces = pieces.reshape(peers, 2, A_DEV, features)
    wide = pieces.transpose(1, 2, 0, 3).reshape(2, A_DEV * peers, features)

    partial_value = jnp.einsum("kd,jd->kj", wide[0], up_b, preferred_element_type=jnp.float32)
    partial_value = partial_value + jnp.einsum(
        "kd,jd->kj", wide[1], gate_b, preferred_element_type=jnp.float32
    )
    gate_rows = pick(gate_b, asked)
    gate_rows, partial_value = lax.optimization_barrier((gate_rows, partial_value))
    terms = cols_reduce(partial_value.reshape(cols, -1, row_count))

    cut = features * 3 // 4 // 128 * 128
    left_rows = pick(down_b[:, :cut], asked)
    right_rows = pick(down_b[:, cut:], asked)

    gate_moved = exchange(gate_rows)
    up_mean = mix(up_a, pick(up_moved, slot))
    tied = lax.optimization_barrier((left_rows, right_rows, up_mean) + tuple(terms[1::2]))
    left_rows, right_rows, up_mean = tied[:3]
    terms[1::2] = tied[3:]
    left = exchange(left_rows)
    gate_mean = mix(gate_a, pick(gate_moved, slot))
    total = terms[0]
    for term in terms[1:]:
        total = total + term
    costs_out = (total * cost_scale).T
    right_rows, gate_mean, costs_out = lax.optimization_barrier((right_rows, gate_mean, costs_out))
    right = exchange(right_rows)
    left_mean = mix(down_a[:, :cut], pick(left, slot))
    down_mean = lax.pad(left_mean, jnp.zeros((), left_mean.dtype), ((0, 0, 0), (0, features - cut, 0)))
    right, down_mean = lax.optimization_barrier((right, down_mean))
    right_mean = mix(down_a[:, cut:], pick(right, slot))
    down_mean = lax.dynamic_update_slice(down_mean, right_mean, (0, cut))
    return (costs_out, up_mean, gate_mean, down_mean)


def solution(mesh):
    placed = (P("rows", "cols"),) * 6 + (P("rows"),)
    return jax.shard_map(
        local,
        mesh=mesh,
        in_specs=placed,
        out_specs=(P("rows", "cols"),) * 4,
        check_vma=False,
    )
```
